32 devices in a mesh: aux: 8 (over z, y), ao: 4 (over x, core).
Axes of the slice: x: 2, y: 2, z: 4, core: 2. Of those that a mesh axis runs over, the one named last changes fastest.
Arguments:
- three_centre: bfloat16 [512, 256, 512], P('aux', 'ao'), may hold values from -6 to 6
- metric: bfloat16 [512, 512], P('aux'), may hold values from -0.25 to 0.25
- density: bfloat16 [256, 64], P('ao'), may hold values from -0.001953125 to 0.001953125
- schwarz: int32 [8, 4], P(None, 'ao'), may hold values 0 or 1
- density_pattern: int32 [16, 4], P('ao'), may hold values 0 or 1
- owner: int32 [8], replicated, may hold values from 0 to 7, as said below
Outputs:
- exchange_blocks: float32 [16, 4096], P('aux', 'ao')
The draws below stay inside these ranges and needn't reach their ends.
Inputs may be any that keep to these rules, and one draw needn't show every extreme that they name: No owner holds more than 2 row tiles, and some owner holds exactly 2. `schwarz`: 1 marks a significant tile. `density_pattern`: 1 marks a nonzero density sub-block.
All inputs are finite; a program needn't handle non-finite values. No bound on the sum of `schwarz` on one device may be relied on, other than what follows from the above.
Results may differ from the reference program's by a relative error of at most 0.0034.
Values may be sent and summed in bfloat16 or wider, within the bound.
No kernel may reach another device: no remote copies, remote signals or barrier semaphores. Data moves between devices by JAX's collectives and lax.ppermute only.
A program may use at most 192 MiB of HBM per device.

```python
import jax
import jax.numpy as jnp
from jax import lax

TILE = 64
RT_DEV = 1
NAUX = 512
CAP = 2
NRT = 8
NROW = 512
NCT = 4
NCOL = 256
N_AUX = 8


def draw_owner(key, part):
    first_key, second_key, third_key = jax.random.split(key, 3)
    owner_count = NRT // RT_DEV
    slot_total = owner_count * CAP
    shuffled = jax.random.permutation(first_key, slot_total).astype(jnp.int32)
    slot_ids = jnp.arange(slot_total, dtype=jnp.int32)
    position = jnp.zeros((slot_total,), jnp.int32).at[shuffled].set(slot_ids)
    busiest = jax.random.randint(second_key, (), 0, owner_count).astype(jnp.int32)
    score = jnp.where(slot_ids // CAP == busiest, slot_ids % CAP, CAP + position)
    order_ids = jnp.argsort(score).astype(jnp.int32)
    chosen = order_ids[:NRT]
    tile_order = jax.random.permutation(third_key, NRT).astype(jnp.int32)
    return (chosen[tile_order] // CAP).astype(jnp.int32)


def place_ends(values, key, least, largest):
    shape = values.shape
    place = [jax.random.randint(jax.random.fold_in(key, axis), (), 0, shape[axis]) for axis in range(len(shape))]
    values = values.at[tuple(place)].set(least)
    longest = shape.index(max(shape))
    place[longest] = (place[longest] + 1) % shape[longest]
    return values.at[tuple(place)].set(largest)


def levels(key, extent, cuts, low, top_value):
    level = 1.0
    for axis_at, shards_of in cuts:
        steps = jax.random.uniform(jax.random.fold_in(jax.random.fold_in(key, 6), axis_at), (shards_of,), jnp.float32, low / len(cuts), top_value / len(cuts))
        level = level * jnp.repeat(jnp.exp(steps), extent[axis_at] // shards_of).reshape((-1,) + (1,) * (len(extent) - 1 - axis_at))
    return level


def centred(stream_key, extent, deviation, reach, pieces=(), kind=jnp.bfloat16):
    entries = deviation * jax.random.normal(stream_key, extent, jnp.float32)
    if pieces:
        entries = entries * levels(stream_key, extent, pieces, -0.22, 0.18)
    return jnp.clip(entries, -reach, reach).astype(kind)


def setup_inputs(seed: int = 0) -> dict:
    splits = jax.random.split(jax.random.key(seed), 7)
    three_centre = centred(splits[0], (NAUX, NCOL, NROW), 1.0, 6.0, ((0, 8), (1, 4)))
    metric = centred(splits[1], (NAUX, NAUX), NAUX ** -0.5, 0.25, ((0, 8),))
    density = centred(splits[2], (NCOL, TILE), (TILE * TILE * NAUX * NCT) ** -0.5, 0.001953125, ((0, 4),))
    schwarz = place_ends((jax.random.randint(splits[3], (NRT, NCT), 0, 4) < 3).astype(jnp.int32), jax.random.fold_in(splits[3], 1), 0, 1)
    density_pattern = place_ends((jax.random.randint(splits[4], (NCT * 4, 4), 0, 4) < 3).astype(jnp.int32), jax.random.fold_in(splits[4], 1), 0, 1)
    owner = draw_owner(jax.random.fold_in(splits[6], 71), 0)
    return {"three_centre": three_centre, "metric": metric, "density": density, "schwarz": schwarz, "density_pattern": density_pattern, "owner": owner}


def exchange_terms(fitted, masked_density):
    tile_size = masked_density.shape[0]
    group_count = fitted.shape[2] // tile_size
    mixed_terms = jnp.einsum("sl,qsm->qlm", masked_density.astype(jnp.float32), fitted.astype(jnp.float32)).astype(jnp.bfloat16)
    left_side = mixed_terms.reshape(-1, group_count, tile_size).astype(jnp.float32)
    right_side = fitted.reshape(-1, group_count, tile_size).astype(jnp.float32)
    blocks = jnp.einsum("xcm,xcn->cmn", left_side, right_side)
    return blocks.reshape(group_count, tile_size * tile_size)


def owner_targets(owner, capacity):
    tile_ids = jnp.arange(owner.shape[0], dtype=jnp.int32)
    same_owner = (owner[:, None] == owner[None, :]) & (tile_ids[None, :] < tile_ids[:, None])
    slot_index = jnp.sum(same_owner.astype(jnp.int32), axis=1).astype(jnp.int32)
    return (owner * capacity + slot_index).astype(jnp.int32)


def reference(three_centre, metric, density, schwarz, density_pattern, owner):
    tile_size = TILE
    sub_block = tile_size // 4
    keep_rows = jnp.repeat(schwarz, tile_size, axis=0)
    pattern = jnp.repeat(jnp.repeat(density_pattern, sub_block, axis=0), sub_block, axis=1)
    masked_density = density * pattern.astype(jnp.bfloat16)

    def one_slab(slab_index):
        slab_data = lax.dynamic_slice_in_dim(three_centre, slab_index * tile_size, tile_size, 1)
        keep_slab = lax.dynamic_slice_in_dim(keep_rows, slab_index, 1, 1)[:, 0].astype(jnp.bfloat16)
        screened = slab_data * keep_slab[None, None, :]
        fitted = jnp.dot(metric, screened.reshape(NAUX, -1), preferred_element_type=jnp.float32)
        fitted = fitted.astype(jnp.bfloat16).reshape(NAUX, tile_size, NROW)
        slab_density = lax.dynamic_slice_in_dim(masked_density, slab_index * tile_size, tile_size, 0)
        return exchange_terms(fitted, slab_density)

    per_slab = lax.map(one_slab, jnp.arange(NCT, dtype=jnp.int32))
    totals = jnp.sum(per_slab, axis=0)
    target = owner_targets(owner, CAP)
    result = jnp.zeros((N_AUX * CAP, tile_size * tile_size), jnp.float32)
    return result.at[target].set(totals)
```

```python
import functools

import jax
import jax.numpy as jnp
from jax import lax
from jax.experimental import pallas as pl
from jax.experimental.pallas import tpu as pltpu
from jax.sharding import PartitionSpec as P

BF16 = jnp.bfloat16
F32 = jnp.float32
GROUP = 16
CHUNKS = (2, 2)
VMEM_LIMIT = 60 << 20


def matmul(a, b, a_dim, b_dim):
    return lax.dot_general(a, b, (((a_dim,), (b_dim,)), ((), ())), preferred_element_type=F32)


def call(kernel, out_shape, in_specs, out_specs, scratch, flops, moved):
    return pl.pallas_call(
        kernel,
        grid_spec=pltpu.PrefetchScalarGridSpec(
            num_scalar_prefetch=1,
            grid=(1,),
            in_specs=in_specs,
            out_specs=out_specs,
            scratch_shapes=scratch,
        ),
        out_shape=out_shape,
        compiler_params=pltpu.CompilerParams(vmem_limit_bytes=VMEM_LIMIT),
        cost_estimate=pl.CostEstimate(flops=flops, bytes_accessed=moved, transcendentals=0),
    )


ANY = pl.BlockSpec(memory_space=pl.ANY)


def whole(shape):
    return pl.BlockSpec(shape, lambda i, *_: (0,) * len(shape))


def pack_kernel(groups, with_metric, me_ref, *refs):
    count = 1 + int(with_metric)
    x_ref = refs[0]
    outs = refs[count:-1]
    planes = refs[-1]
    part = x_ref.shape[0]
    rows = x_ref.shape[2]
    half = GROUP // 2
    r = lax.broadcasted_iota(jnp.int32, (GROUP * GROUP, GROUP * GROUP), 0)
    c = lax.broadcasted_iota(jnp.int32, (GROUP * GROUP, GROUP * GROUP), 1)
    swap = jnp.where((r // GROUP == c % GROUP) & (r % GROUP == c // GROUP), 1.0, 0.0).astype(BF16)
    low = lax.broadcasted_iota(jnp.int32, (half, part, 128), 2) < 64
    for g in range(groups):
        for pb in range(part // GROUP):
            block = x_ref[pb * GROUP : (pb + 1) * GROUP, g * GROUP : (g + 1) * GROUP, :]
            y = matmul(swap, block.reshape(GROUP * GROUP, rows), 1, 0).astype(BF16)
            planes[:, pb * GROUP : (pb + 1) * GROUP, :] = y.reshape(GROUP, GROUP, rows)
        for k, out in enumerate(outs):
            tile = me_ref[0] ^ k
            odd = (tile % 2) == 1
            lane = pl.multiple_of((tile // 2) * 128, 128)
            first = planes[:half, :, pl.ds(lane, 128)]
            second = planes[half:, :, pl.ds(lane, 128)]
            moved = jnp.where(odd, first, second)
            moved = jnp.concatenate([moved[..., 64:], moved[..., :64]], -1)
            kept = jnp.where(odd, second, first)
            out[g * half : (g + 1) * half] = jnp.where(low == odd, moved, kept)
    if with_metric:
        metric_ref = refs[1]
        for lt in range(metric_ref.shape[1] // 128):
            piece = metric_ref[:, lt * 128 : (lt + 1) * 128]
            for out in outs:
                out[groups * half + lt] = piece


def pack(me, three_centre, metric, first, groups, aux_count):
    part, _, rows = three_centre.shape
    extra = 0 if metric is None else metric.shape[1] // 128
    size = groups * GROUP // 2 + extra
    span = groups * GROUP
    args = [three_centre]
    in_specs = [pl.BlockSpec((pl.Element(part), pl.Element(span), pl.Element(rows)), lambda i, *_: (0, first * GROUP, 0))]
    if metric is not None:
        args.append(metric)
        in_specs.append(whole(metric.shape))
    shape = (size, part, 128)
    return call(
        functools.partial(pack_kernel, groups, metric is not None),
        [jax.ShapeDtypeStruct(shape, BF16)] * aux_count,
        in_specs,
        [whole(shape)] * aux_count,
        [pltpu.VMEM((GROUP, part, rows), BF16)],
        2 * part * span * rows * 256,
        2 * part * span * rows * 2,
    )(me, *args)


def load_blocks(me_ref, blocks, start, size, buffer, sems):
    copies = []
    for k, block in enumerate(blocks):
        part = block.shape[1]
        at = pl.multiple_of((me_ref[0] ^ k) * part, part)
        copy = pltpu.make_async_copy(
            block.at[pl.ds(start, size)], buffer.at[:, pl.ds(at, part), :], sems.at[k]
        )
        copy.start()
        copies.append(copy)
    return copies


def fit(x, metric_t, store, size, tile):
    def body(i, carry):
        pair = jnp.concatenate([x[2 * i], x[2 * i + 1]], axis=1).T
        res = matmul(pair, metric_t[...], 1, 0).astype(BF16)
        half = GROUP // 2
        for j in range(2):
            plane = 2 * i + j
            s = (plane // half) * GROUP + plane % half
            store[s] = res[2 * j * tile : (2 * j + 1) * tile]
            store[s + half] = res[(2 * j + 1) * tile : (2 * j + 2) * tile]
        return carry

    lax.fori_loop(0, size // 2, body, 0)


def first_kernel(count, size, tile, me_ref, *refs):
    blocks = refs[:count]
    fitted, metric_t, x, m, x_sems, m_sems = refs[count:]
    extra = m.shape[0]
    m_copies = load_blocks(me_ref, blocks, size, extra, m, m_sems)
    x_copies = load_blocks(me_ref, blocks, 0, size, x, x_sems)
    for copy in m_copies:
        copy.wait()
    for lt in range(extra):
        metric_t[lt * 128 : (lt + 1) * 128, :] = m[lt].T
    for copy in x_copies:
        copy.wait()
    fit(x, metric_t, fitted, size, tile)


def last_kernel(count, sizes, tile, parts, scal_ref, *refs):
    blocks = refs[:count]
    metric_t, density, earlier, out = refs[count : count + 4]
    fitted, mixed, kron, x, x_sems, f_sem = refs[count + 4 :]
    size = sizes[-1]
    done = sum(sizes[:-1]) * 2
    aux_count, ao_count = parts
    wide = GROUP * tile
    x_copies = load_blocks(scal_ref, blocks, 0, size, x, x_sems)
    f_copy = pltpu.make_async_copy(earlier, fitted.at[pl.ds(0, done)], f_sem)
    f_copy.start()
    r = lax.broadcasted_iota(jnp.int32, (wide, tile), 0)
    c = lax.broadcasted_iota(jnp.int32, (wide, tile), 1)
    spread = jnp.where(r // GROUP == c, 1.0, 0.0).astype(BF16)
    tall = matmul(spread, density[...], 1, 1).astype(BF16)
    full = matmul(tall, spread, 1, 1)
    rr = lax.broadcasted_iota(jnp.int32, (wide, wide), 0) % GROUP
    cc = lax.broadcasted_iota(jnp.int32, (wide, wide), 1) % GROUP
    kron[...] = jnp.where(rr == cc, full, 0.0).astype(BF16)
    for copy in x_copies:
        copy.wait()
    fit(x, metric_t, fitted.at[pl.ds(done, 2 * size)], size, tile)
    f_copy.wait()
    total = fitted.shape[2]
    step = tile // 4
    for g in range(tile // GROUP):
        rhs = fitted[:, g * GROUP : (g + 1) * GROUP, :].reshape(wide, total)
        for h in range(4):
            res = matmul(kron[h * step * GROUP : (h + 1) * step * GROUP, :], rhs, 1, 0)
            mixed[h * step : (h + 1) * step, g * GROUP : (g + 1) * GROUP, :] = res.astype(BF16).reshape(step, GROUP, total)
    block = lax.fori_loop(
        0, tile, lambda l, acc: acc + matmul(mixed[l], fitted[l], 1, 1), jnp.zeros((tile, tile), F32), unroll=8
    )
    block = jnp.where(scal_ref[1] != 0, block, 0.0)
    share = tile // ao_count
    for a in range(ao_count):
        piece = block[a * share : (a + 1) * share]
        piece = jnp.concatenate([piece[: share // 2], piece[share // 2 :]], axis=1)
        for q in range(aux_count):
            out[q * ao_count + a] = piece


def place_kernel(tile_count, ao_count, capacity, tile, scal_ref, got, out):
    half = got.shape[1]
    for slot in range(capacity):
        want = scal_ref[0] * capacity + slot
        total = jnp.zeros(got.shape[1:], F32)
        for t in range(tile_count):
            part = got[t * ao_count]
            for a in range(1, ao_count):
                part = part + got[t * ao_count + a]
            total = total + jnp.where(scal_ref[1 + t] == want, part, 0.0)
        for i in range(half):
            side = 0 if 2 * i < half else tile
            row = 2 * i if 2 * i < half else 2 * i - half
            pair = jnp.concatenate(
                [total[row : row + 1, side : side + tile], total[row + 1 : row + 2, side : side + tile]], axis=1
            )
            out[slot : slot + 1, 2 * i * tile : (2 * i + 2) * tile] = pair


def local(three_centre, metric, density, schwarz, density_pattern, owner):
    part, tile, rows = three_centre.shape
    total = metric.shape[1]
    aux_count = lax.axis_size("aux")
    ao_count = lax.axis_size("ao")
    tile_count = owner.shape[0]
    capacity = 2 * (tile_count // aux_count)
    sub_block = tile // 4
    index = lax.axis_index("aux").astype(jnp.int32)
    me = index[None]

    sizes = [g * GROUP // 2 for g in CHUNKS]
    chunks = []
    first = 0
    for j, groups in enumerate(CHUNKS):
        sent = pack(me, three_centre, metric if j == 0 else None, first, groups, aux_count)
        first += groups
        got = [sent[0]]
        for k in range(1, aux_count):
            got.append(lax.ppermute(sent[k], "aux", [(i, i ^ k) for i in range(aux_count)]))
        chunks.append(got)

    pattern = jnp.repeat(jnp.repeat(density_pattern, sub_block, axis=0), sub_block, axis=1)
    masked_density = density * pattern.astype(BF16)
    keep = lax.dynamic_slice_in_dim(schwarz[:, 0], index, 1, 0)
    tile_ids = jnp.arange(tile_count, dtype=jnp.int32)
    same_owner = (owner[:, None] == owner[None, :]) & (tile_ids[None, :] < tile_ids[:, None])
    target = owner * capacity + jnp.sum(same_owner.astype(jnp.int32), axis=1)

    extra = total // 128
    size = sizes[0]
    fitted, metric_t = call(
        functools.partial(first_kernel, aux_count, size, tile),
        [jax.ShapeDtypeStruct((2 * size, tile, total), BF16), jax.ShapeDtypeStruct((total, total), BF16)],
        [ANY] * aux_count,
        [whole((2 * size, tile, total)), whole((total, total))],
        [
            pltpu.VMEM((size, total, 128), BF16),
            pltpu.VMEM((extra, total, 128), BF16),
            pltpu.SemaphoreType.DMA((aux_count,)),
            pltpu.SemaphoreType.DMA((aux_count,)),
        ],
        2 * total * total * 2 * size * tile,
        2 * total * 2 * size * tile * 2,
    )(me, *chunks[0])

    size = sizes[1]
    share = tile // ao_count
    out_shape = (aux_count * ao_count, share // 2, 2 * tile)
    blocks = call(
        functools.partial(last_kernel, aux_count, sizes, tile, (aux_count, ao_count)),
        jax.ShapeDtypeStruct(out_shape, F32),
        [ANY] * aux_count + [whole((total, total)), whole((tile, tile)), ANY],
        whole(out_shape),
        [
            pltpu.VMEM((tile, tile, total), BF16),
            pltpu.VMEM((tile, tile, total), BF16),
            pltpu.VMEM((GROUP * tile, GROUP * tile), BF16),
            pltpu.VMEM((size, total, 128), BF16),
            pltpu.SemaphoreType.DMA((aux_count,)),
            pltpu.SemaphoreType.DMA(()),
        ],
        4 * total * total * 2 * size * tile,
        2 * total * 2 * size * tile * 2,
    )(jnp.concatenate([me, keep]), *chunks[1], metric_t, masked_density, fitted)

    got = lax.all_to_all(blocks, ("aux", "ao"), split_axis=0, concat_axis=0, tiled=True)
    out_shape = (capacity, tile * tile // ao_count)
    return call(
        functools.partial(place_kernel, tile_count, ao_count, capacity, tile),
        jax.ShapeDtypeStruct(out_shape, F32),
        [whole(got.shape)],
        whole(out_shape),
        [],
        0,
        got.size * 4,
    )(jnp.concatenate([me, target]), got)


def solution(mesh):
    return jax.shard_map(
        local,
        mesh=mesh,
        in_specs=(
            P("aux", "ao", None),
            P("aux", None),
            P("ao", None),
            P(None, "ao"),
            P("ao", None),
            P(),
        ),
        out_specs=P("aux", "ao"),
        check_vma=False,
    )
```

```python
import functools

import jax
import jax.numpy as jnp
from jax import lax
from jax.experimental import pallas as pl
from jax.experimental.pallas import tpu as pltpu
from jax.sharding import PartitionSpec as P

BF16 = jnp.bfloat16
F32 = jnp.float32
GROUP = 16
HELD = 3


ANY = pl.BlockSpec(memory_space=pl.ANY)


def matmul(a, b, a_dim, b_dim):
    return lax.dot_general(a, b, (((a_dim,), (b_dim,)), ((), ())), preferred_element_type=F32)


def whole(shape):
    return pl.BlockSpec(shape, lambda i, *_: (0,) * len(shape))


def call(kernel, out_shape, in_specs, out_specs, scratch, limit, flops, moved):
    return pl.pallas_call(
        kernel,
        grid_spec=pltpu.PrefetchScalarGridSpec(
            num_scalar_prefetch=1,
            grid=(1,),
            in_specs=in_specs,
            out_specs=out_specs,
            scratch_shapes=scratch,
        ),
        out_shape=out_shape,
        compiler_params=pltpu.CompilerParams(vmem_limit_bytes=limit),
        cost_estimate=pl.CostEstimate(flops=flops, bytes_accessed=moved, transcendentals=0),
    )


def pack_kernel(groups, first_partner, local_tiles, me_ref, *refs):
    x_ref = refs[0]
    planes = refs[-1]
    with_metric = len(refs) > local_tiles + 2
    outs = refs[1 + int(with_metric) : -1]
    part = x_ref.shape[0]
    lanes = x_ref.shape[2]
    half = GROUP // 2
    r = lax.broadcasted_iota(jnp.int32, (GROUP * GROUP, GROUP * GROUP), 0)
    c = lax.broadcasted_iota(jnp.int32, (GROUP * GROUP, GROUP * GROUP), 1)
    swap = jnp.where((r // GROUP == c % GROUP) & (r % GROUP == c // GROUP), 1.0, 0.0).astype(BF16)
    low = lax.broadcasted_iota(jnp.int32, (half, part, 128), 2) < 64
    for g in range(groups):
        for pb in range(part // GROUP):
            block = x_ref[pb * GROUP : (pb + 1) * GROUP, g * GROUP : (g + 1) * GROUP, :]
            y = matmul(swap, block.reshape(GROUP * GROUP, lanes), 1, 0).astype(BF16)
            planes[:, pb * GROUP : (pb + 1) * GROUP, :] = y.reshape(GROUP, GROUP, lanes)
        for k, out in enumerate(outs):
            tile = (me_ref[0] ^ (first_partner + k)) % local_tiles
            odd = (tile % 2) == 1
            lane = pl.multiple_of((tile // 2) * 128, 128)
            first = planes[:half, :, pl.ds(lane, 128)]
            second = planes[half:, :, pl.ds(lane, 128)]
            moved = jnp.where(odd, first, second)
            moved = jnp.concatenate([moved[..., 64:], moved[..., :64]], -1)
            kept = jnp.where(odd, second, first)
            out[g * half : (g + 1) * half] = jnp.where(low == odd, moved, kept)
    if with_metric:
        metric_ref = refs[1]
        share = metric_ref.shape[0]
        for lt in range(metric_ref.shape[1] // 128):
            piece = metric_ref[:, lt * 128 : (lt + 1) * 128]
            for out in outs:
                out[groups * half, lt * share : (lt + 1) * share, :] = piece


def pack(scal, three_centre, metric, share, first, groups, far, aux_count):
    part, _, rows = three_centre.shape
    near = aux_count // 2
    lanes = rows // 2
    span = groups * GROUP
    size = span // 2 + (0 if metric is None else 1)
    args = [three_centre]
    in_specs = [
        pl.BlockSpec(
            (pl.Element(part), pl.Element(span), pl.Element(lanes)),
            lambda i, sc: (0, first * GROUP, ((sc[0] // near) ^ int(far)) * lanes),
        )
    ]
    if metric is not None:
        args.append(metric)
        in_specs.append(pl.BlockSpec((share, metric.shape[1]), lambda i, sc: (sc[1], 0)))
    shape = (size, part, 128)
    return call(
        functools.partial(pack_kernel, groups, near if far else 0, near),
        [jax.ShapeDtypeStruct(shape, BF16)] * near,
        in_specs,
        [whole(shape)] * near,
        [pltpu.VMEM((GROUP, part, lanes), BF16)],
        24 << 20,
        2 * part * span * lanes * 256,
        2 * part * span * lanes * 2,
    )(scal, *args)


def load_blocks(me_ref, blocks, starts, size, buffer, sems):
    copies = []
    for k, block in enumerate(blocks):
        part = block.shape[1]
        at = pl.multiple_of((me_ref[0] ^ k) * part, part)
        copy = pltpu.make_async_copy(
            block.at[pl.ds(starts[k], size)], buffer.at[:, pl.ds(at, part), :], sems.at[k]
        )
        copy.start()
        copies.append(copy)
    return copies


def fit(x, metric_t, store, size, tile):
    half = GROUP // 2

    def body(i, carry):
        pair = jnp.concatenate([x[2 * i], x[2 * i + 1]], axis=1).T
        res = matmul(pair, metric_t[...], 1, 0).astype(BF16)
        for j in range(2):
            plane = 2 * i + j
            s = (plane // half) * GROUP + plane % half
            store[s] = res[2 * j * tile : (2 * j + 1) * tile]
            store[s + half] = res[(2 * j + 1) * tile : (2 * j + 2) * tile]
        return carry

    lax.fori_loop(0, size // 2, body, 0)


def spread_out(block):
    rows, columns = block.shape
    r = lax.broadcasted_iota(jnp.int32, (rows * GROUP, rows), 0)
    c = lax.broadcasted_iota(jnp.int32, (rows * GROUP, rows), 1)
    tall = matmul(jnp.where(r // GROUP == c, 1.0, 0.0).astype(BF16), block, 1, 0).astype(BF16)
    r = lax.broadcasted_iota(jnp.int32, (columns, columns * GROUP), 0)
    c = lax.broadcasted_iota(jnp.int32, (columns, columns * GROUP), 1)
    full = matmul(tall, jnp.where(c // GROUP == r, 1.0, 0.0).astype(BF16), 1, 0)
    rr = lax.broadcasted_iota(jnp.int32, full.shape, 0) % GROUP
    cc = lax.broadcasted_iota(jnp.int32, full.shape, 1) % GROUP
    return jnp.where(rr == cc, full, 0.0).astype(BF16)


def rows_of(planes, g):
    piece = planes[:, g * GROUP : (g + 1) * GROUP, :]
    return piece.reshape(piece.shape[0] * GROUP, piece.shape[2])


def contract(left, left_first, right, count, start):
    return lax.fori_loop(
        0, count, lambda l, acc: acc + matmul(left[left_first + l], right[l], 1, 1), start, unroll=8
    )


def first_kernel(count, starts, size, tile, scal_ref, *refs):
    blocks = refs[:count]
    shares = refs[count:-13]
    density, density_t, metric_t, cross_l, cross_s, block = refs[-13:-7]
    fitted, mixed, kron, kron_s, m, x, sems = refs[-7:]
    copies = load_blocks(scal_ref, blocks, starts, size, x, sems)
    share_planes = shares[0].shape[0]
    tiles = m.shape[0]
    step = shares[0].shape[1] // tiles
    for j, share in enumerate(shares):
        for k in range(share_planes):
            at = (j * share_planes + k) * step
            for lt in range(tiles):
                m[lt, at : at + step, :] = share[k, lt * step : (lt + 1) * step, :]
    for lt in range(tiles):
        metric_t[lt * 128 : (lt + 1) * 128, :] = m[lt].T
    held = 2 * size
    kron[...] = spread_out(density_t[:, :held])
    kron_s[...] = spread_out(density[held:, :held])
    for copy in copies:
        copy.wait()
    fit(x, metric_t, fitted, size, tile)
    total = fitted.shape[2]
    rest = tile - held
    for g in range(tile // GROUP):
        at = slice(g * GROUP, (g + 1) * GROUP)
        rhs = rows_of(fitted, g)
        for h in range(tile // GROUP):
            res = matmul(kron[h * GROUP * GROUP : (h + 1) * GROUP * GROUP, :], rhs, 1, 0)
            res = res.astype(BF16).reshape(GROUP, GROUP, total)
            if h * GROUP < held:
                mixed[h * GROUP : (h + 1) * GROUP, at, :] = res
            else:
                cross_l[h * GROUP - held : (h + 1) * GROUP - held, at, :] = res
        res = matmul(kron_s[...], rhs, 1, 0)
        cross_s[:, at, :] = res.astype(BF16).reshape(rest, GROUP, total)
    block[...] = contract(mixed, 0, fitted, held, jnp.zeros((tile, tile), F32))


def last_kernel(count, starts, size, tile, parts, scal_ref, *refs):
    blocks = refs[:count]
    metric_t, density_t, cross_l, cross_s, before, out = refs[count : count + 6]
    fitted, mixed, x, sems = refs[count + 6 :]
    aux_count, ao_count = parts
    copies = load_blocks(scal_ref, blocks, starts, size, x, sems)
    rest = 2 * size
    kron = spread_out(density_t[tile - rest :, tile - rest :])
    for copy in copies:
        copy.wait()
    fit(x, metric_t, fitted, size, tile)
    total = fitted.shape[2]
    block = contract(fitted, 0, cross_s, rest, before[...])
    for g in range(tile // GROUP):
        at = slice(g * GROUP, (g + 1) * GROUP)
        res = matmul(kron, rows_of(fitted, g), 1, 0).reshape(rest, GROUP, total)
        mixed[:, at, :] = (res + cross_l[:, at, :].astype(F32)).astype(BF16)
    block = contract(mixed, 0, fitted, rest, block)
    block = jnp.where(scal_ref[2] != 0, block, 0.0)
    share = tile // ao_count
    for a in range(ao_count):
        piece = block[a * share : (a + 1) * share]
        piece = jnp.concatenate([piece[: share // 2], piece[share // 2 :]], axis=1)
        for q in range(aux_count):
            out[q * ao_count + a] = piece


def place_kernel(tile_count, ao_count, capacity, tile, scal_ref, got, out):
    half = got.shape[1]
    for slot in range(capacity):
        want = scal_ref[0] * capacity + slot
        total = jnp.zeros(got.shape[1:], F32)
        for t in range(tile_count):
            part = got[t * ao_count]
            for a in range(1, ao_count):
                part = part + got[t * ao_count + a]
            total = total + jnp.where(scal_ref[1 + t] == want, part, 0.0)
        for i in range(half):
            side = 0 if 2 * i < half else tile
            row = 2 * i if 2 * i < half else 2 * i - half
            pair = jnp.concatenate(
                [total[row : row + 1, side : side + tile], total[row + 1 : row + 2, side : side + tile]], axis=1
            )
            out[slot : slot + 1, 2 * i * tile : (2 * i + 2) * tile] = pair


def local(three_centre, metric, density, schwarz, density_pattern, owner):
    part, tile, rows = three_centre.shape
    total = metric.shape[1]
    aux_count = lax.axis_size("aux")
    ao_count = lax.axis_size("ao")
    tile_count = owner.shape[0]
    capacity = 2 * (tile_count // aux_count)
    sub_block = tile // 4
    near = aux_count // 2
    index = lax.axis_index("aux").astype(jnp.int32)
    keep = lax.dynamic_slice_in_dim(schwarz[:, 0], index, 1, 0)
    scal = jnp.stack([index, lax.axis_index("ao").astype(jnp.int32)])
    scal_keep = jnp.concatenate([scal, keep])

    groups = tile // GROUP
    share = part // ao_count
    far_first = pack(scal, three_centre, metric, share, 0, HELD, True, aux_count)
    near_all = pack(scal, three_centre, metric, share, 0, groups, False, aux_count)
    far_last = pack(scal, three_centre, None, share, HELD, groups - HELD, True, aux_count)

    def swap(x, k):
        return lax.ppermute(x, "aux", [(i, i ^ k) for i in range(aux_count)])

    far_first = [swap(x, near + k) for k, x in enumerate(far_first)]
    near_all = [near_all[0]] + [swap(x, k) for k, x in enumerate(near_all) if k]
    far_last = [swap(x, near + k) for k, x in enumerate(far_last)]

    pattern = jnp.repeat(jnp.repeat(density_pattern, sub_block, axis=0), sub_block, axis=1)
    masked_density = density * pattern.astype(BF16)
    masked_density_t = masked_density.T
    tile_ids = jnp.arange(tile_count, dtype=jnp.int32)
    same_owner = (owner[:, None] == owner[None, :]) & (tile_ids[None, :] < tile_ids[:, None])
    target = owner * capacity + jnp.sum(same_owner.astype(jnp.int32), axis=1)

    own_share = jnp.stack([x[-1] for x in near_all + far_first])
    shares = [own_share]
    for j in range(1, ao_count):
        shares.append(lax.ppermute(own_share, "ao", [(i, i ^ j) for i in range(ao_count)]))

    size = HELD * GROUP // 2
    rest = (groups - HELD) * GROUP
    planes = jax.ShapeDtypeStruct((rest, tile, total), BF16)
    metric_t, cross_l, cross_s, block = call(
        functools.partial(first_kernel, aux_count, (0,) * aux_count, size, tile),
        [jax.ShapeDtypeStruct((total, total), BF16), planes, planes, jax.ShapeDtypeStruct((tile, tile), F32)],
        [ANY] * aux_count + [whole(own_share.shape)] * ao_count + [whole((tile, tile))] * 2,
        [whole((total, total)), whole(planes.shape), whole(planes.shape), whole((tile, tile))],
        [
            pltpu.VMEM((2 * size, tile, total), BF16),
            pltpu.VMEM((2 * size, tile, total), BF16),
            pltpu.VMEM((GROUP * tile, GROUP * 2 * size), BF16),
            pltpu.VMEM((GROUP * rest, GROUP * 2 * size), BF16),
            pltpu.VMEM((total // 128, total, 128), BF16),
            pltpu.VMEM((size, total, 128), BF16),
            pltpu.SemaphoreType.DMA((aux_count,)),
        ],
        total * (48 << 10),
        2 * total * total * 2 * size * tile,
        2 * total * 2 * size * tile * 2,
    )(scal, *near_all, *far_first, *shares, masked_density, masked_density_t)

    rows_out = tile // ao_count
    out_shape = (aux_count * ao_count, rows_out // 2, 2 * tile)
    blocks = call(
        functools.partial(
            last_kernel, aux_count, (size,) * near + (0,) * near, rest // 2, tile, (aux_count, ao_count)
        ),
        jax.ShapeDtypeStruct(out_shape, F32),
        [ANY] * aux_count
        + [whole((total, total)), whole((tile, tile)), whole(planes.shape), whole(planes.shape), whole((tile, tile))],
        whole(out_shape),
        [
            pltpu.VMEM((rest, tile, total), BF16),
            pltpu.VMEM((rest, tile, total), BF16),
            pltpu.VMEM((rest // 2, total, 128), BF16),
            pltpu.SemaphoreType.DMA((aux_count,)),
        ],
        total * (28 << 10),
        2 * total * total * rest * tile,
        2 * total * rest * tile * 2,
    )(scal_keep, *near_all, *far_last, metric_t, masked_density_t, cross_l, cross_s, block)

    got = lax.all_to_all(blocks, ("aux", "ao"), split_axis=0, concat_axis=0, tiled=True)
    out_shape = (capacity, tile * tile // ao_count)
    return call(
        functools.partial(place_kernel, tile_count, ao_count, capacity, tile),
        jax.ShapeDtypeStruct(out_shape, F32),
        [whole(got.shape)],
        whole(out_shape),
        [],
        4 << 20,
        0,
        got.size * 4,
    )(jnp.concatenate([index[None], target]), got)


def solution(mesh):
    return jax.shard_map(
        local,
        mesh=mesh,
        in_specs=(
            P("aux", "ao", None),
            P("aux", None),
            P("ao", None),
            P(None, "ao"),
            P("ao", None),
            P(),
        ),
        out_specs=P("aux", "ao"),
        check_vma=False,
    )
```
